256 devices in a mesh: seq: 8 (over z), exp: 16 (over y, x), edp: 2 (over core).
Axes of the slice: x: 4, y: 4, z: 8, core: 2. Of those that a mesh axis runs over, the one named last changes fastest.
Arguments:
- tokens: bfloat16 [32768, 2048], P(('seq', 'exp', 'edp')), may hold values from -6 to 6
- route_ids: int32 [32768, 8], P(('seq', 'exp', 'edp')), may hold values from 0 to 127, all different within a row; in each aligned block of 128 rows (0 to 127, 128 to 255, ...) at most 9 rows name the same one
- gates: float32 [32768, 8], P(('seq', 'exp', 'edp')), may hold values from 0.05 to 0.5
- d_out: bfloat16 [32768, 2048], P(('seq', 'exp', 'edp')), may hold values from -6 to 6
- w_gate: bfloat16 [128, 2048, 384], P(('seq', 'exp')), may hold values from -0.125 to 0.125
- w_up: bfloat16 [128, 2048, 384], P(('seq', 'exp')), may hold values from -0.125 to 0.125
- w_down: bfloat16 [128, 2048, 384], P(('seq', 'exp')), may hold values from -0.3125 to 0.3125
Outputs:
- d_tokens: bfloat16 [32768, 2048], P(('seq', 'exp', 'edp'))
- grad_gate: float32 [128, 2048, 384], P(('seq', 'exp'), 'edp')
- grad_up: float32 [128, 2048, 384], P(('seq', 'exp'), 'edp')
- grad_down: float32 [128, 2048, 384], P(('seq', 'exp'), 'edp')
The draws below stay inside these ranges and needn't reach their ends.
Inputs may be any that keep to these rules, and one draw needn't show every extreme that they name: `route_ids`: among the 128 tokens of one device no expert is named more than 9 times, a bound that some block reaches; a token names 8 different experts.
All inputs are finite; a program needn't handle non-finite values.
Results may differ from the reference program's by a relative error of at most 0.0064.
Values may be sent and summed in bfloat16 or wider, within the bound.
No kernel may reach another device: no remote copies, remote signals or barrier semaphores. Data moves between devices by JAX's collectives and lax.ppermute only.
A program may use at most 128 MiB of HBM per device.

```python
import math
import jax
import jax.numpy as jnp
import numpy as np
from jax import lax

D = 2048
HID = 384
TOPK = 8
TOK_DEV = 128
EXPERTS = 128
CAP = 9
TOKENS = 32768
N_SEQ = 8
N_EXP = 16
N_EDP = 2


def level_of(rng, extent, pieces, low, high):
    def one(axis_at, parts):
        heights = jax.random.uniform(jax.random.fold_in(jax.random.fold_in(rng, 6), axis_at), (parts,), jnp.float32, low / len(pieces), high / len(pieces))
        return jnp.repeat(jnp.exp(heights), extent[axis_at] // parts).reshape((-1,) + (1,) * (len(extent) - axis_at - 1))

    level = one(*pieces[0])
    for cut in pieces[1:]:
        level = level * one(*cut)
    return level


def deal_out(own_key, own, number, rows, count, top, bound, skew):
    ranking = jax.random.permutation(own_key, count)
    crowded, usual = load_shares(count, rows * top, bound, skew, True), load_shares(count, rows * top, bound, skew, False)
    places = jnp.arange(count)

    def named(lengths, rotation):
        used = int((lengths > 0).sum())
        fixed = max(1, used // 4)
        shifted = fixed + (places - fixed + rotation * (used - fixed)) % max(1, count - fixed)
        return jnp.zeros((count,), jnp.int32).at[ranking[jnp.where(places < fixed, places, shifted)]].set(jnp.asarray(lengths, jnp.int32))

    lengths = jnp.where(number % 4 == 0, named(crowded, number // 4), named(usual, number - number // 4 - 1))
    mixed = jax.random.permutation(jax.random.fold_in(own, 3), count)
    source_of, sink = mixed[0:count // 2 * 2:2], mixed[1:count // 2 * 2:2]
    slack = jnp.minimum(lengths[source_of] - 1, bound - lengths[sink]) // 2
    slack = jnp.where((source_of == ranking[0]) | (sink == ranking[0]) | (lengths[sink] == 0), 0, jnp.maximum(slack, 0))
    shifted = jax.random.randint(jax.random.fold_in(own, 4), (count // 2,), 0, 1 << 20) % (slack + 1)
    lengths = lengths.at[source_of].add(-shifted).at[sink].add(shifted)
    labels = jnp.searchsorted(jnp.cumsum(lengths), jnp.arange(rows * top), side="right").astype(jnp.int32)
    listing = labels.reshape(top, rows).T
    listing = listing[jax.random.permutation(jax.random.fold_in(own, 1), rows)]
    rotation = jax.random.randint(jax.random.fold_in(own, 2), (rows, 1), 0, top)
    return jnp.take_along_axis(listing, (jnp.arange(top)[None, :] + rotation) % top, axis=1)


def load_shares(number_of, total, bound, slope, full):
    portions = [(1 << 20) // math.isqrt(rank ** slope) + 1 for rank in range(1, number_of + 1)]
    largest = bound if full else min(bound, max(-(-total // number_of), total * portions[0] // sum(portions)))
    least = 1 if total - largest >= number_of - 1 else 0
    holding, surplus = [largest] + [least] * (number_of - 1), total - largest - least * (number_of - 1)
    while surplus > 0:
        candidates = [i for i in range(1, number_of) if holding[i] < largest] or [i for i in range(1, number_of) if holding[i] < bound]
        pool, left = sum([portions[i] for i in candidates]), surplus
        for i in candidates:
            extra = min(bound - holding[i], max(1, left * portions[i] // pool), surplus)
            holding[i] = holding[i] + extra
            surplus = surplus - extra
    return np.array(holding)


def scatter_about(own_key, dims, scale, reach, cuts=(), kind=jnp.bfloat16):
    gain = level_of(own_key, dims, cuts, -0.22, 0.18) if cuts else 1.0
    array = jax.random.normal(own_key, dims, jnp.float32) * scale * gain
    return jnp.minimum(jnp.maximum(array, -reach), reach).astype(kind)


def setup_inputs(seed: int = 0) -> dict:
    streams_of = jax.random.split(jax.random.key(seed), 8)
    tokens = scatter_about(streams_of[0], (TOKENS, D), 1.0, 6.0, ((0, 256),))
    route_ids_keys = jax.random.split(jax.random.fold_in(streams_of[1], 1), TOKENS // TOK_DEV)
    route_ids_turns = jax.random.permutation(jax.random.fold_in(streams_of[1], 3), TOKENS // TOK_DEV)
    route_ids = jax.vmap(lambda own, number: deal_out(jax.random.fold_in(streams_of[1], 2), own, number, TOK_DEV, EXPERTS, TOPK, CAP, 1))(route_ids_keys, route_ids_turns).reshape((TOKENS, TOPK))
    gates = jnp.clip(jnp.exp(math.log(0.5) - 2.3025851 * jax.random.uniform(streams_of[2], (TOKENS, TOPK), jnp.float32) ** level_of(streams_of[2], (TOKENS, TOPK), ((0, 256),), -0.2, 0.2)), 0.05, 0.5)
    d_out = scatter_about(streams_of[3], (TOKENS, D), 1.0, 6.0, ((0, 256),))
    w_gate = scatter_about(streams_of[4], (EXPERTS, D, HID), D ** -0.5, 0.125, ((0, 128),))
    w_up = scatter_about(streams_of[5], (EXPERTS, D, HID), D ** -0.5, 0.125, ((0, 128),))
    w_down = scatter_about(streams_of[6], (EXPERTS, D, HID), HID ** -0.5, 0.3125, ((0, 128),))
    return dict(tokens=tokens, route_ids=route_ids, gates=gates, d_out=d_out, w_gate=w_gate, w_up=w_up, w_down=w_down)


def expert_grads(x_rows, dy_rows, wg, wu, wd):
    a = jnp.dot(x_rows, wg, preferred_element_type=jnp.float32)
    b = jnp.dot(x_rows, wu, preferred_element_type=jnp.float32)
    sig = jax.nn.sigmoid(a)
    act = a * sig
    hidden = (act * b).astype(jnp.bfloat16)
    d_hidden = jnp.dot(dy_rows, wd, preferred_element_type=jnp.float32)
    d_gate = (d_hidden * b * sig * (1.0 + a * (1.0 - sig))).astype(jnp.bfloat16)
    d_upper = (d_hidden * act).astype(jnp.bfloat16)
    contract_one = (((1,), (1,)), ((), ()))
    contract_zero = (((0,), (0,)), ((), ()))
    back = lax.dot_general(d_gate, wg, contract_one, preferred_element_type=jnp.float32)
    back = back + lax.dot_general(d_upper, wu, contract_one, preferred_element_type=jnp.float32)
    grad_g = lax.dot_general(x_rows, d_gate, contract_zero, preferred_element_type=jnp.float32)
    grad_u = lax.dot_general(x_rows, d_upper, contract_zero, preferred_element_type=jnp.float32)
    grad_d = lax.dot_general(dy_rows, hidden, contract_zero, preferred_element_type=jnp.float32)
    return back.astype(jnp.bfloat16), grad_g, grad_u, grad_d


def reference(tokens, route_ids, gates, d_out, w_gate, w_up, w_down):
    topk = route_ids.shape[1]
    most = N_SEQ * N_EXP * N_EDP * CAP
    flat_ids = route_ids.reshape(-1)
    flat_gates = gates.reshape(-1)

    def per_expert(carry, expert):
        chosen = flat_ids == expert
        where_rows = jnp.nonzero(chosen, size=most, fill_value=0)[0].astype(jnp.int32)
        count = jnp.sum(chosen.astype(jnp.int32))
        valid = (jnp.arange(most, dtype=jnp.int32) < count)[:, None]
        owner = (where_rows // topk).astype(jnp.int32)
        x_rows = jnp.where(valid, tokens[owner], 0.0).astype(jnp.bfloat16)
        scaled = flat_gates[where_rows][:, None] * d_out[owner].astype(jnp.float32)
        dy_rows = jnp.where(valid, scaled, 0.0).astype(jnp.bfloat16)
        back, grad_g, grad_u, grad_d = expert_grads(x_rows, dy_rows, w_gate[expert], w_up[expert], w_down[expert])
        carry = carry.at[owner].add(jnp.where(valid, back.astype(jnp.float32), 0.0))
        return carry, (grad_g, grad_u, grad_d)

    start = jnp.zeros((tokens.shape[0], tokens.shape[1]), jnp.float32)
    total, grads = lax.scan(per_expert, start, jnp.arange(EXPERTS, dtype=jnp.int32))
    return total.astype(jnp.bfloat16), grads[0], grads[1], grads[2]
```

```python
import jax
import jax.numpy as jnp
from jax import lax
from jax.sharding import PartitionSpec as P


F32 = jnp.float32
BF16 = jnp.bfloat16


def ring_perms(count):
    up = [(i, (i + 1) % count) for i in range(count)]
    down = [(i, (i - 1) % count) for i in range(count)]
    return up, down


def ring_gather(block, count):
    up, down = ring_perms(count)
    rows = block.shape[0]
    half = count // 2
    from_low, from_high = block, block
    low, high = [], []
    for _ in range(half - 1):
        from_low = lax.ppermute(from_low, "seq", up)
        from_high = lax.ppermute(from_high, "seq", down)
        low.append(from_low)
        high.append(from_high)
    mid_low = lax.ppermute(from_low[: rows // 2], "seq", up)
    mid_high = lax.ppermute(from_high[rows // 2 :], "seq", down)
    return jnp.concatenate([block] + low + [mid_low, mid_high] + high[::-1], axis=0)


def ring_scatter(part, count):
    up, down = ring_perms(count)
    half = count // 2
    rows = part.shape[1]
    mid = rows // 2
    to_low = lax.ppermute(part[half, :mid].astype(BF16), "seq", down)
    to_high = lax.ppermute(part[half, mid:].astype(BF16), "seq", up)
    for step in range(half - 1, 0, -1):
        low, high = part[step], part[count - step]
        if step == half - 1:
            low = jnp.concatenate([low[:mid] + to_low.astype(F32), low[mid:]])
            high = jnp.concatenate([high[:mid], high[mid:] + to_high.astype(F32)])
        else:
            low = low + to_low.astype(F32)
            high = high + to_high.astype(F32)
        to_low = lax.ppermute(low.astype(BF16), "seq", down)
        to_high = lax.ppermute(high.astype(BF16), "seq", up)
    return (part[0] + to_low.astype(F32) + to_high.astype(F32)).astype(BF16)


def on_device(tokens, route_ids, gates, d_out, w_gate, w_up, w_down):
    tok_count, width = tokens.shape
    topk = route_ids.shape[1]
    n_seq = lax.axis_size("seq")
    n_exp = lax.axis_size("exp")
    experts = n_seq * n_exp
    pairs = tok_count * topk
    cap = pairs // experts + max(1, pairs // (8 * experts))
    slots = cap * n_seq
    rows = n_exp * slots
    table = n_seq * tok_count
    z = lax.axis_index("seq")
    half = width // 2

    meta = jnp.concatenate([route_ids.T.astype(F32), gates.T], axis=0)
    meta = jnp.broadcast_to(meta[None], (n_seq,) + meta.shape)
    meta = lax.all_to_all(meta, "seq", 0, 0, tiled=True)
    x_tab = [ring_gather(tokens[:, :half], n_seq), ring_gather(tokens[:, half:], n_seq)]
    d_tab = [ring_gather(d_out[:, :half], n_seq), ring_gather(d_out[:, half:], n_seq)]

    meta = meta[::-1]
    meta = lax.dynamic_slice_in_dim(jnp.concatenate([meta, meta]), n_seq - 1 - z, n_seq)
    ids, gate = meta[:, :topk], meta[:, topk:]
    mine = (z * n_exp + jnp.arange(n_exp, dtype=jnp.int32)).astype(F32)
    match = ids[:, None] == mine[None, :, None, None]
    named = jnp.any(match, axis=2).astype(F32)
    gate = jnp.sum(jnp.where(match, gate[:, None], 0.0), axis=2)
    place = jnp.arange(tok_count)
    before = (place[:, None] < place[None, :]).astype(BF16)
    rank = jnp.einsum("zet,tu->zeu", named.astype(BF16), before, preferred_element_type=F32)
    first = (cap * jnp.arange(n_seq)).astype(F32)[:, None, None]
    code = jnp.where(named > 0, rank + first, -1.0)
    code = jnp.transpose(code, (1, 0, 2)).reshape(n_exp, 1, table)
    gate = jnp.transpose(gate, (1, 0, 2)).reshape(n_exp, 1, table)
    hit = code == jnp.arange(slots).astype(F32)[None, :, None]
    gate_slot = jnp.sum(jnp.where(hit, gate, 0.0), axis=2).reshape(rows, 1)
    pick = hit.astype(BF16).reshape(rows, table)

    def exchange(block):
        block = block.reshape(n_exp, slots, block.shape[-1])
        return lax.all_to_all(block, "exp", 0, 0, tiled=True).reshape(rows, block.shape[-1])

    x = [exchange(jnp.dot(pick, t, preferred_element_type=F32).astype(BF16)) for t in x_tab]
    dy = [
        exchange((jnp.dot(pick, t, preferred_element_type=F32) * gate_slot).astype(BF16))
        for t in d_tab
    ]

    wg, wu, wd = w_gate[0], w_up[0], w_down[0]

    def project(parts, w):
        return sum(
            jnp.dot(p, w[i * half : (i + 1) * half], preferred_element_type=F32)
            for i, p in enumerate(parts)
        )

    a = project(x, wg)
    b = project(x, wu)
    sig = jax.nn.sigmoid(a)
    act = a * sig
    hidden = (act * b).astype(BF16)
    d_hidden = project(dy, wd)
    d_gate = (d_hidden * b * sig * (1.0 + a * (1.0 - sig))).astype(BF16)
    d_upper = (d_hidden * act).astype(BF16)
    contract_one = (((1,), (1,)), ((), ()))
    contract_zero = (((0,), (0,)), ((), ()))
    outs = []
    for i in range(2):
        cols = slice(i * half, (i + 1) * half)
        back = lax.dot_general(d_gate, wg[cols], contract_one, preferred_element_type=F32)
        back = back + lax.dot_general(d_upper, wu[cols], contract_one, preferred_element_type=F32)
        back = exchange(back.astype(BF16))
        part = lax.dot_general(pick, back, contract_zero, preferred_element_type=F32)
        outs.append(ring_scatter(part.reshape(n_seq, tok_count, half), n_seq))
    d_tokens = jnp.concatenate(outs, axis=1)

    core = lax.axis_index("edp")
    swap = [(0, 1), (1, 0)]

    def shared_grad(parts, right):
        grad = jnp.concatenate(
            [lax.dot_general(p, right, contract_zero, preferred_element_type=F32) for p in parts]
        )
        other = lax.dynamic_slice_in_dim(grad, (1 - core) * half, half)
        own = lax.dynamic_slice_in_dim(grad, core * half, half)
        return (own + lax.ppermute(other, "edp", swap))[None]

    return (d_tokens, shared_grad(x, d_gate), shared_grad(x, d_upper), shared_grad(dy, hidden))


def solution(mesh):
    tok = P(("seq", "exp", "edp"), None)
    wts = P(("seq", "exp"), None, None)
    out = P(("seq", "exp"), "edp", None)
    return jax.shard_map(
        on_device,
        mesh=mesh,
        in_specs=(tok, tok, tok, tok, wts, wts, wts),
        out_specs=(tok, out, out, out),
        check_vma=False,
    )
```

```python
import jax
import jax.numpy as jnp
from jax import lax
from jax.experimental import pallas as pl
from jax.experimental.pallas import tpu as pltpu
from jax.sharding import PartitionSpec as P


F32 = jnp.float32
BF16 = jnp.bfloat16


def whole(shape):
    return pl.BlockSpec(shape, lambda *_: (0,) * len(shape))


def ring_perms(count):
    up = [(i, (i + 1) % count) for i in range(count)]
    down = [(i, (i - 1) % count) for i in range(count)]
    return up, down


def shift(value, perm, axis="seq"):
    return lax.ppermute(value, axis, perm)


def ring_gather(block, count):
    up, down = ring_perms(count)
    rows = block.shape[0]
    half = count // 2
    from_low, from_high = block, block
    low, high = [], []
    for _ in range(1, half):
        from_low = shift(from_low, up)
        from_high = shift(from_high, down)
        low.append(from_low)
        high.append(from_high)
    mid_low = shift(from_low[: rows // 2], up)
    mid_high = shift(from_high[rows // 2 :], down)
    return [block] + low + [mid_low, mid_high] + high[::-1]


def ring_scatter(part, count):
    up, down = ring_perms(count)
    half = count // 2
    mid = part.shape[1] // 2

    def plus(mine, came):
        return (mine.astype(F32) + came.astype(F32)).astype(BF16)

    to_low = shift(part[half, :mid], down)
    to_high = shift(part[half, mid:], up)
    for step in range(half - 1, 0, -1):
        low, high = part[step], part[count - step]
        if step == half - 1:
            low = jnp.concatenate([plus(low[:mid], to_low), low[mid:]])
            high = jnp.concatenate([high[:mid], plus(high[mid:], to_high)])
        else:
            low, high = plus(low, to_low), plus(high, to_high)
        low, high = lax.optimization_barrier((low, high))
        to_low = shift(low, down)
        to_high = shift(high, up)
    total = part[0].astype(F32) + to_low.astype(F32) + to_high.astype(F32)
    return total.astype(BF16)


def index_tables(meta, z, n_exp, cap):
    n_seq, double, tok = meta.shape
    topk = double // 2
    slots = cap * n_seq
    chunk = 16
    per_pair = 2 * slots // chunk

    def body(z_ref, meta_ref, pick_ref, gate_ref, code_s, weight_s):
        own = z_ref[0]
        expert = (lax.broadcasted_iota(jnp.int32, (n_exp, tok), 0) + n_exp * own).astype(F32)
        before = lax.broadcasted_iota(jnp.int32, (tok, tok), 0) < lax.broadcasted_iota(
            jnp.int32, (tok, tok), 1
        )
        before = before.astype(F32).astype(BF16)
        for p in range(n_seq):
            source = jnp.where(own >= p, own - p, own - p + n_seq)
            block = meta_ref[source]
            named = jnp.zeros((n_exp, tok), F32)
            weight = jnp.zeros((n_exp, tok), F32)
            for k in range(topk):
                hit = block[k : k + 1, :] == expert
                named = jnp.where(hit, 1.0, named)
                weight = jnp.where(hit, block[topk + k : topk + k + 1, :], weight)
            rank = jnp.dot(named.astype(BF16), before, preferred_element_type=F32)
            code = jnp.where(named > 0.0, rank + float(cap * p), -1.0)
            code_s[:, p * tok : (p + 1) * tok] = code
            weight_s[:, p * tok : (p + 1) * tok] = weight

        def pair(i, carry):
            first = code_s[pl.ds(2 * i, 1), :]
            second = code_s[pl.ds(2 * i + 1, 1), :]
            second = jnp.where(second < 0.0, -1.0, second + float(slots))
            w_first = weight_s[pl.ds(2 * i, 1), :]
            w_second = weight_s[pl.ds(2 * i + 1, 1), :]
            row = lax.broadcasted_iota(jnp.int32, (chunk, n_seq * tok), 0).astype(F32)
            for c in range(per_pair):
                here = row + float(c * chunk)
                hit_a = here == first
                hit_b = here == second
                at = pl.ds(pl.multiple_of(i * 2 * slots + c * chunk, chunk), chunk)
                pick_ref[at, :] = jnp.where(hit_a | hit_b, 1.0, 0.0).astype(BF16)
                weight = jnp.where(hit_a, w_first, 0.0) + jnp.where(hit_b, w_second, 0.0)
                gate_ref[at, :] = jnp.sum(weight, axis=1, keepdims=True)
            return carry

        lax.fori_loop(0, n_exp // 2, pair, 0)

    return pl.pallas_call(
        body,
        grid=(1,),
        in_specs=[pl.BlockSpec(memory_space=pltpu.SMEM), whole(meta.shape)],
        out_specs=[whole((n_exp * slots, n_seq * tok)), whole((n_exp * slots, 1))],
        out_shape=[
            jax.ShapeDtypeStruct((n_exp * slots, n_seq * tok), BF16),
            jax.ShapeDtypeStruct((n_exp * slots, 1), F32),
        ],
        scratch_shapes=[pltpu.VMEM((n_exp, n_seq * tok), F32)] * 2,
    )(z.reshape(1), meta)


def pick_rows(pick, pieces, cols, first=0, gate=None, block=256):
    rows = pick.shape[0]
    first = first // block

    def body(*refs):
        out = refs[-1]
        parts = refs[1 : 1 + len(pieces)]
        tab = jnp.concatenate([r[...] for r in parts], axis=0)
        got = jnp.dot(refs[0][...], tab, preferred_element_type=F32)
        if gate is not None:
            got = got * refs[-2][...]
        out[...] = got.astype(BF16)

    extra = [] if gate is None else [gate]
    return pl.pallas_call(
        body,
        grid=(cols // block,),
        in_specs=[whole(pick.shape)]
        + [pl.BlockSpec((p.shape[0], block), lambda j: (0, j + first)) for p in pieces]
        + [whole(g.shape) for g in extra],
        out_specs=pl.BlockSpec((rows, block), lambda j: (0, j)),
        out_shape=jax.ShapeDtypeStruct((rows, cols), BF16),
    )(pick, *pieces, *extra)


def project(x0, x1, w, block=384):
    rows, half = x0.shape
    wide = w.shape[1]

    def body(x0_ref, x1_ref, w_ref, o_ref):
        got = jnp.dot(x0_ref[...], w_ref[:half], preferred_element_type=F32)
        o_ref[...] = got + jnp.dot(x1_ref[...], w_ref[half:], preferred_element_type=F32)

    row = lambda width: pl.BlockSpec((block, width), lambda i: (i, 0))
    return pl.pallas_call(
        body,
        grid=(rows // block,),
        in_specs=[row(half), row(half), whole(w.shape)],
        out_specs=row(wide),
        out_shape=jax.ShapeDtypeStruct((rows, wide), F32),
    )(x0, x1, w)


def hidden_part(d0, wd, block=384):
    rows, half = d0.shape
    hid = wd.shape[1]

    def body(d_ref, w_ref, o_ref):
        o_ref[...] = jnp.dot(d_ref[...], w_ref[...], preferred_element_type=F32)

    row = lambda width: pl.BlockSpec((block, width), lambda i: (i, 0))
    return pl.pallas_call(
        body,
        grid=(rows // block,),
        in_specs=[row(half), pl.BlockSpec((half, hid), lambda i: (0, 0))],
        out_specs=row(hid),
        out_shape=jax.ShapeDtypeStruct((rows, hid), F32),
    )(d0, wd)


BACK_DIMS = (((1,), (1,)), ((), ()))


def middle(d1, dh0, wd, ab, w, block=384):
    rows, half = d1.shape
    hid = wd.shape[1]

    def body(d1_ref, dh_ref, wd_ref, ab_ref, w_ref, h_ref, dab_ref, back_ref):
        dh = dh_ref[...] + jnp.dot(d1_ref[...], wd_ref[...], preferred_element_type=F32)
        a, b = ab_ref[:, :hid], ab_ref[:, hid:]
        sig = jax.nn.sigmoid(a)
        act = a * sig
        h_ref[...] = (act * b).astype(BF16)
        da = (dh * b * sig * (1.0 + a * (1.0 - sig))).astype(BF16)
        db = (dh * act).astype(BF16)
        dab_ref[:, :hid] = da
        dab_ref[:, hid:] = db
        got = lax.dot_general(da, w_ref[:, :hid], BACK_DIMS, preferred_element_type=F32)
        got = got + lax.dot_general(db, w_ref[:, hid:], BACK_DIMS, preferred_element_type=F32)
        back_ref[...] = got.astype(BF16)

    row = lambda width: pl.BlockSpec((block, width), lambda i: (i, 0))
    return pl.pallas_call(
        body,
        grid=(rows // block,),
        in_specs=[
            row(half),
            row(hid),
            pl.BlockSpec((half, hid), lambda i: (1, 0)),
            row(2 * hid),
            pl.BlockSpec((half, 2 * hid), lambda i: (0, 0)),
        ],
        out_specs=[row(hid), row(2 * hid), row(half)],
        out_shape=[
            jax.ShapeDtypeStruct((rows, hid), BF16),
            jax.ShapeDtypeStruct((rows, 2 * hid), BF16),
            jax.ShapeDtypeStruct((rows, half), BF16),
        ],
    )(d1, dh0, wd, ab, w)


def back_rows(dab, w, which, block=384):
    rows, wide = dab.shape
    half = w.shape[0] // 2

    def body(d_ref, w_ref, o_ref):
        got = lax.dot_general(d_ref[...], w_ref[...], BACK_DIMS, preferred_element_type=F32)
        o_ref[...] = got.astype(BF16)

    row = lambda width: pl.BlockSpec((block, width), lambda i: (i, 0))
    return pl.pallas_call(
        body,
        grid=(rows // block,),
        in_specs=[row(wide), pl.BlockSpec((half, wide), lambda i: (which, 0))],
        out_specs=row(half),
        out_shape=jax.ShapeDtypeStruct((rows, half), BF16),
    )(dab, w)


def across(left, right, kind, block=256):
    rows, cols = left.shape
    dims = (((0,), (0,)), ((), ()))

    def body(l_ref, r_ref, o_ref):
        got = lax.dot_general(l_ref[...], r_ref[...], dims, preferred_element_type=F32)
        o_ref[...] = got.astype(kind)

    return pl.pallas_call(
        body,
        grid=(cols // block,),
        in_specs=[pl.BlockSpec((rows, block), lambda j: (0, j)), whole(right.shape)],
        out_specs=pl.BlockSpec((block, right.shape[1]), lambda j: (j, 0)),
        out_shape=jax.ShapeDtypeStruct((cols, right.shape[1]), kind),
    )(left, right)


def on_device(tokens, route_ids, gates, d_out, w_gate, w_up, w_down):
    tok_count, width = tokens.shape
    topk = route_ids.shape[1]
    n_seq = lax.axis_size("seq")
    n_exp = lax.axis_size("exp")
    experts = n_seq * n_exp
    pairs = tok_count * topk
    cap = pairs // experts + max(1, pairs // (8 * experts))
    slots = cap * n_seq
    rows = n_exp * slots
    z = lax.axis_index("seq")
    core = lax.axis_index("edp")
    half = width // 2

    def exchange(block):
        block = block.reshape(n_exp, slots, block.shape[-1])
        got = lax.all_to_all(block, "exp", 0, 0, tiled=True)
        return got.reshape(rows, got.shape[-1])

    meta = jnp.concatenate([route_ids.T.astype(F32), gates.T], axis=0)
    meta = jnp.broadcast_to(meta[None], (n_seq,) + meta.shape)
    meta = lax.all_to_all(meta, "seq", 0, 0, tiled=True)
    tabs = {
        "x0": (ring_gather(tokens[:, :half], n_seq), 0),
        "x1": (ring_gather(tokens[:, half:], n_seq), 0),
    }
    pieces = ring_gather(d_out, n_seq)
    tabs["d0"] = (pieces, 0)
    tabs["d1"] = (pieces, half)
    pick, gate = index_tables(meta, z, n_exp, cap)
    got = {}
    for name, (pieces, first) in tabs.items():
        send = pick_rows(pick, pieces, half, first, gate if name[0] == "d" else None)
        got[name] = exchange(send)
    w = jnp.concatenate([w_gate[0], w_up[0]], axis=1)
    wd = w_down[0]
    ab = project(got["x0"], got["x1"], w)
    dh0 = hidden_part(got["d0"], wd)
    hidden, d_both, back0 = middle(got["d1"], dh0, wd, ab, w)
    back1 = back_rows(d_both, w, 1)
    outs = []
    for back in (back0, back1):
        back = exchange(back)
        part = across(pick, back, BF16)
        outs.append(ring_scatter(part.reshape(n_seq, tok_count, half), n_seq))
    d_tokens = jnp.concatenate(outs, axis=1)

    def shared_grad(name, right):
        low = across(got[name + "0"], right, F32)
        high = across(got[name + "1"], right, F32)
        other = jnp.where(core == 0, high, low)
        own = jnp.where(core == 0, low, high)
        return own + shift(other, [(0, 1), (1, 0)], "edp")

    grad_d = shared_grad("d", hidden)
    grad_gu = shared_grad("x", d_both)
    hid = wd.shape[1]
    return (d_tokens, grad_gu[None, :, :hid], grad_gu[None, :, hid:], grad_d[None])


def solution(mesh):
    tok = P(("seq", "exp", "edp"), None)
    wts = P(("seq", "exp"), None, None)
    out = P(("seq", "exp"), "edp", None)

    return jax.shard_map(
        on_device,
        mesh=mesh,
        in_specs=(tok, tok, tok, tok, wts, wts, wts),
        out_specs=(tok, out, out, out),
        check_vma=False,
    )
```

```python
import jax
import jax.numpy as jnp
from jax import lax
from jax.experimental import pallas as pl
from jax.experimental.pallas import tpu as pltpu
from jax.sharding import PartitionSpec as P


F32 = jnp.float32
BF16 = jnp.bfloat16


def whole(shape):
    return pl.BlockSpec(shape, lambda *_: (0,) * len(shape))


def ring_perms(count):
    up = [(i, (i + 1) % count) for i in range(count)]
    down = [(i, (i - 1) % count) for i in range(count)]
    return up, down


def shift(value, perm, axis="seq"):
    return lax.ppermute(value, axis, perm)


def ring_gather(block, count, split):
    up, down = ring_perms(count)
    mid = block.shape[0] // 2
    half = count // 2
    from_low, from_high = block, block
    low, high = [], []
    for _ in range(1, half):
        from_low = shift(from_low, up)
        from_high = shift(from_high, down)
        low.append(from_low)
        high.append(from_high)
    if split:
        far = [shift(from_low[:mid], up), shift(from_high[mid:], down)]
    else:
        far = [shift(from_low, up)]
    return [block] + low + far + high[::-1]


def ring_scatter(part, count, split):
    up, down = ring_perms(count)
    half = count // 2
    mid = part.shape[1] // 2

    def plus(mine, came):
        return (mine.astype(F32) + came.astype(F32)).astype(BF16)

    if split:
        to_low = shift(part[half, :mid], down)
        to_high = shift(part[half, mid:], up)
    else:
        to_low = shift(part[half], down)
    for step in range(half - 1, 0, -1):
        low, high = part[step], part[count - step]
        if step < half - 1:
            low, high = plus(low, to_low), plus(high, to_high)
        elif split:
            low = jnp.concatenate([plus(low[:mid], to_low), low[mid:]])
            high = jnp.concatenate([high[:mid], plus(high[mid:], to_high)])
        else:
            low = plus(low, to_low)
        low, high = lax.optimization_barrier((low, high))
        to_low = shift(low, down)
        to_high = shift(high, up)
    total = part[0].astype(F32) + to_low.astype(F32) + to_high.astype(F32)
    return total.astype(BF16)


def index_tables(meta, z, n_exp, cap):
    n_seq, double, tok = meta.shape
    topk = double // 2
    slots = cap * n_seq
    chunk = 16
    per_pair = 2 * slots // chunk

    def body(z_ref, meta_ref, pick_ref, gate_ref, code_s, weight_s):
        own = z_ref[0]
        expert = (lax.broadcasted_iota(jnp.int32, (n_exp, tok), 0) + n_exp * own).astype(F32)
        before = lax.broadcasted_iota(jnp.int32, (tok, tok), 0) < lax.broadcasted_iota(
            jnp.int32, (tok, tok), 1
        )
        before = before.astype(F32).astype(BF16)
        for p in range(n_seq):
            source = jnp.where(own >= p, own - p, own - p + n_seq)
            block = meta_ref[source]
            named = jnp.zeros((n_exp, tok), F32)
            weight = jnp.zeros((n_exp, tok), F32)
            for k in range(topk):
                hit = block[k : k + 1, :] == expert
                named = jnp.where(hit, 1.0, named)
                weight = jnp.where(hit, block[topk + k : topk + k + 1, :], weight)
            rank = jnp.dot(named.astype(BF16), before, preferred_element_type=F32)
            code = jnp.where(named > 0.0, rank + float(cap * p), -1.0)
            code_s[:, p * tok : (p + 1) * tok] = code
            weight_s[:, p * tok : (p + 1) * tok] = weight

        def pair(i, carry):
            first = code_s[pl.ds(2 * i, 1), :]
            second = code_s[pl.ds(2 * i + 1, 1), :]
            second = jnp.where(second < 0.0, -1.0, second + float(slots))
            w_first = weight_s[pl.ds(2 * i, 1), :]
            w_second = weight_s[pl.ds(2 * i + 1, 1), :]
            row = lax.broadcasted_iota(jnp.int32, (chunk, n_seq * tok), 0).astype(F32)
            for c in range(per_pair):
                here = row + float(c * chunk)
                hit_a = here == first
                hit_b = here == second
                at = pl.ds(pl.multiple_of(i * 2 * slots + c * chunk, chunk), chunk)
                pick_ref[at, :] = jnp.where(hit_a | hit_b, 1.0, 0.0).astype(BF16)
                weight = jnp.where(hit_a, w_first, 0.0) + jnp.where(hit_b, w_second, 0.0)
                gate_ref[at, :] = jnp.sum(weight, axis=1, keepdims=True)
            return carry

        lax.fori_loop(0, n_exp // 2, pair, 0)

    return pl.pallas_call(
        body,
        grid=(1,),
        in_specs=[pl.BlockSpec(memory_space=pltpu.SMEM), whole(meta.shape)],
        out_specs=[whole((n_exp * slots, n_seq * tok)), whole((n_exp * slots, 1))],
        out_shape=[
            jax.ShapeDtypeStruct((n_exp * slots, n_seq * tok), BF16),
            jax.ShapeDtypeStruct((n_exp * slots, 1), F32),
        ],
        scratch_shapes=[pltpu.VMEM((n_exp, n_seq * tok), F32)] * 2,
    )(z.reshape(1), meta)


def pick_rows(pick, pieces, cols, which=0, gate=None, block=384, step=256):
    rows, table = pick.shape
    starts = [sum(p.shape[0] for p in pieces[:i]) for i in range(len(pieces))]

    def body(*refs):
        out, tab = refs[-2:]

        @pl.when(pl.program_id(0) == 0)
        def _():
            for r, at in zip(refs[1 : 1 + len(pieces)], starts):
                tab[at : at + r.shape[0], :] = r[...]

        def part(c, carry):
            at = pl.ds(pl.multiple_of(c * step, step), step)
            got = jnp.dot(refs[0][...], tab[:, at], preferred_element_type=F32)
            if gate is not None:
                got = got * refs[-3][...]
            out[:, at] = got.astype(BF16)
            return carry

        lax.fori_loop(0, cols // step, part, 0)

    row = lambda width: pl.BlockSpec((block, width), lambda i: (i, 0))
    return pl.pallas_call(
        body,
        grid=(rows // block,),
        in_specs=[row(table)]
        + [pl.BlockSpec((p.shape[0], cols), lambda i: (0, which)) for p in pieces]
        + ([] if gate is None else [row(1)]),
        out_specs=row(cols),
        out_shape=jax.ShapeDtypeStruct((rows, cols), BF16),
        scratch_shapes=[pltpu.VMEM((table, cols), BF16)],
    )(pick, *pieces, *([] if gate is None else [gate]))


def project(x0, x1, w, block=192):
    rows, half = x0.shape
    wide = w.shape[1]

    def body(x0_ref, x1_ref, w_ref, o_ref):
        got = jnp.dot(x0_ref[...], w_ref[:half], preferred_element_type=F32)
        o_ref[...] = got + jnp.dot(x1_ref[...], w_ref[half:], preferred_element_type=F32)

    row = lambda width: pl.BlockSpec((block, width), lambda i: (i, 0))
    return pl.pallas_call(
        body,
        grid=(rows // block,),
        in_specs=[row(half), row(half), whole(w.shape)],
        out_specs=row(wide),
        out_shape=jax.ShapeDtypeStruct((rows, wide), F32),
    )(x0, x1, w)


def hidden_part(d0, wd, block=192):
    rows, half = d0.shape
    hid = wd.shape[1]

    def body(d_ref, w_ref, o_ref):
        o_ref[...] = jnp.dot(d_ref[...], w_ref[...], preferred_element_type=F32)

    row = lambda width: pl.BlockSpec((block, width), lambda i: (i, 0))
    return pl.pallas_call(
        body,
        grid=(rows // block,),
        in_specs=[row(half), pl.BlockSpec((half, hid), lambda i: (0, 0))],
        out_specs=row(hid),
        out_shape=jax.ShapeDtypeStruct((rows, hid), F32),
    )(d0, wd)


BACK_DIMS = (((1,), (1,)), ((), ()))


def middle(d1, dh0, wd, ab, w, block=384):
    rows, half = d1.shape
    hid = wd.shape[1]

    def body(d1_ref, dh_ref, wd_ref, ab_ref, w_ref, h_ref, dab_ref, back_ref):
        dh = dh_ref[...] + jnp.dot(d1_ref[...], wd_ref[...], preferred_element_type=F32)
        a, b = ab_ref[:, :hid], ab_ref[:, hid:]
        sig = jax.nn.sigmoid(a)
        act = a * sig
        h_ref[...] = (act * b).astype(BF16)
        da = (dh * b * sig * (1.0 + a * (1.0 - sig))).astype(BF16)
        db = (dh * act).astype(BF16)
        dab_ref[:, :hid] = da
        dab_ref[:, hid:] = db
        got = lax.dot_general(da, w_ref[:, :hid], BACK_DIMS, preferred_element_type=F32)
        got = got + lax.dot_general(db, w_ref[:, hid:], BACK_DIMS, preferred_element_type=F32)
        back_ref[...] = got.astype(BF16)

    row = lambda width: pl.BlockSpec((block, width), lambda i: (i, 0))
    return pl.pallas_call(
        body,
        grid=(rows // block,),
        in_specs=[
            row(half),
            row(hid),
            pl.BlockSpec((half, hid), lambda i: (1, 0)),
            row(2 * hid),
            pl.BlockSpec((half, 2 * hid), lambda i: (0, 0)),
        ],
        out_specs=[row(hid), row(2 * hid), row(half)],
        out_shape=[
            jax.ShapeDtypeStruct((rows, hid), BF16),
            jax.ShapeDtypeStruct((rows, 2 * hid), BF16),
            jax.ShapeDtypeStruct((rows, half), BF16),
        ],
    )(d1, dh0, wd, ab, w)


def back_rows(dab, w, which, block=192):
    rows, wide = dab.shape
    half = w.shape[0] // 2

    def body(d_ref, w_ref, o_ref):
        got = lax.dot_general(d_ref[...], w_ref[...], BACK_DIMS, preferred_element_type=F32)
        o_ref[...] = got.astype(BF16)

    row = lambda width: pl.BlockSpec((block, width), lambda i: (i, 0))
    return pl.pallas_call(
        body,
        grid=(rows // block,),
        in_specs=[row(wide), pl.BlockSpec((half, wide), lambda i: (which, 0))],
        out_specs=row(half),
        out_shape=jax.ShapeDtypeStruct((rows, half), BF16),
    )(dab, w)


def combine(left, right, block=256):
    rows, cols = left.shape
    dims = (((0,), (0,)), ((), ()))

    def body(l_ref, r_ref, o_ref):
        got = lax.dot_general(l_ref[...], r_ref[...], dims, preferred_element_type=F32)
        o_ref[...] = got.astype(BF16)

    return pl.pallas_call(
        body,
        grid=(cols // block,),
        in_specs=[pl.BlockSpec((rows, block), lambda j: (0, j)), whole(right.shape)],
        out_specs=pl.BlockSpec((block, right.shape[1]), lambda j: (j, 0)),
        out_shape=jax.ShapeDtypeStruct((cols, right.shape[1]), BF16),
    )(left, right)


def weight_grads(core, x0, x1, d0, d1, dab, h, block=256):
    rows, half = x0.shape
    wide = dab.shape[1]
    total = wide + h.shape[1]
    n = half // block
    dims = (((0,), (0,)), ((), ()))

    def place(j, core_ref):
        return lax.rem(j + (1 - core_ref[0]) * n, 2 * n)

    def body(core_ref, x0_ref, x1_ref, d0_ref, d1_ref, dab_ref, h_ref, other_ref, own_ref, s_ref):
        j = pl.program_id(0)
        at = place(j, core_ref)

        def fill(x_ref, d_ref):
            s_ref[0] = x_ref[...]
            s_ref[1] = d_ref[...]

        pl.when(at < n)(lambda: fill(x0_ref, d0_ref))
        pl.when(at >= n)(lambda: fill(x1_ref, d1_ref))
        ab = lax.dot_general(s_ref[0], dab_ref[...], dims, preferred_element_type=F32)
        down = lax.dot_general(s_ref[1], h_ref[...], dims, preferred_element_type=F32)

        def put(o_ref):
            o_ref[:, :wide] = ab
            o_ref[:, wide:] = down

        pl.when(j < n)(lambda: put(other_ref))
        pl.when(j >= n)(lambda: put(own_ref))

    low = pl.BlockSpec((rows, block), lambda j, c: (0, jnp.minimum(place(j, c), n - 1)))
    high = pl.BlockSpec((rows, block), lambda j, c: (0, jnp.maximum(place(j, c) - n, 0)))
    return pl.pallas_call(
        body,
        grid_spec=pltpu.PrefetchScalarGridSpec(
            num_scalar_prefetch=1,
            grid=(2 * n,),
            in_specs=[low, high, low, high, whole(dab.shape), whole(h.shape)],
            out_specs=[
                pl.BlockSpec((block, total), lambda j, c: (jnp.minimum(j, n - 1), 0)),
                pl.BlockSpec((block, total), lambda j, c: (jnp.maximum(j - n, 0), 0)),
            ],
            scratch_shapes=[pltpu.VMEM((2, rows, block), BF16)],
        ),
        out_shape=[jax.ShapeDtypeStruct((half, total), F32)] * 2,
    )(core.reshape(1), x0, x1, d0, d1, dab, h)


def finish_grads(own, came, hid, block=128):
    rows, total = own.shape

    def body(own_ref, came_ref, *outs):
        for i, o_ref in enumerate(outs):
            cols = slice(i * hid, (i + 1) * hid)
            o_ref[...] = own_ref[:, cols] + came_ref[:, cols]

    row = lambda width: pl.BlockSpec((block, width), lambda i: (i, 0))
    return pl.pallas_call(
        body,
        grid=(rows // block,),
        in_specs=[row(total), row(total)],
        out_specs=[row(hid)] * (total // hid),
        out_shape=[jax.ShapeDtypeStruct((rows, hid), F32)] * (total // hid),
    )(own, came)


def on_device(tokens, route_ids, gates, d_out, w_gate, w_up, w_down):
    tok_count, width = tokens.shape
    topk = route_ids.shape[1]
    n_seq = lax.axis_size("seq")
    n_exp = lax.axis_size("exp")
    experts = n_seq * n_exp
    pairs = tok_count * topk
    cap = pairs // experts + max(1, pairs // (8 * experts))
    slots = cap * n_seq
    rows = n_exp * slots
    z = lax.axis_index("seq")
    core = lax.axis_index("edp")
    half = width // 2

    def exchange(block):
        block = block.reshape(n_exp, slots, block.shape[-1])
        got = lax.all_to_all(block, "exp", 0, 0, tiled=True)
        return got.reshape(rows, got.shape[-1])

    meta = jnp.concatenate([route_ids.T.astype(F32), gates.T], axis=0)
    meta = jnp.broadcast_to(meta[None], (n_seq,) + meta.shape)
    meta = lax.all_to_all(meta, "seq", 0, 0, tiled=True)
    tabs = {
        "x0": (ring_gather(tokens[:, :half], n_seq, True), 0),
        "x1": (ring_gather(tokens[:, half:], n_seq, False), 0),
    }
    pieces = ring_gather(d_out, n_seq, False)
    tabs["d0"] = (pieces, 0)
    tabs["d1"] = (pieces, 1)
    pick, gate = index_tables(meta, z, n_exp, cap)
    got = {}
    for name, (pieces, which) in tabs.items():
        send = pick_rows(pick, pieces, half, which, gate if name[0] == "d" else None)
        got[name] = exchange(send)
    w = jnp.concatenate([w_gate[0], w_up[0]], axis=1)
    wd = w_down[0]
    ab = project(got["x0"], got["x1"], w)
    dh0 = hidden_part(got["d0"], wd)
    hidden, d_both, back0 = middle(got["d1"], dh0, wd, ab, w)
    back1 = back_rows(d_both, w, 1)
    outs = []
    for i, back in enumerate((back0, back1)):
        back = exchange(back)
        part = combine(pick, back)
        outs.append(ring_scatter(part.reshape(n_seq, tok_count, half), n_seq, i == 1))
    d_tokens = jnp.concatenate(outs, axis=1)

    other, own = weight_grads(core, got["x0"], got["x1"], got["d0"], got["d1"], d_both, hidden)
    came = shift(other, [(0, 1), (1, 0)], "edp")
    grads = finish_grads(own, came, wd.shape[1])
    return (d_tokens, grads[0][None], grads[1][None], grads[2][None])


def solution(mesh):
    tok = P(("seq", "exp", "edp"), None)
    wts = P(("seq", "exp"), None, None)
    out = P(("seq", "exp"), "edp", None)

    return jax.shard_map(
        on_device,
        mesh=mesh,
        in_specs=(tok, tok, tok, tok, wts, wts, wts),
        out_specs=(tok, out, out, out),
        check_vma=False,
    )
```

```python
import jax
import jax.numpy as jnp
from jax import lax
from jax.experimental import pallas as pl
from jax.experimental.pallas import tpu as pltpu
from jax.sharding import PartitionSpec as P


F32 = jnp.float32
BF16 = jnp.bfloat16


def whole(shape):
    return pl.BlockSpec(shape, lambda *_: (0,) * len(shape))


def ring_perms(count):
    up = [(i, (i + 1) % count) for i in range(count)]
    down = [(i, (i - 1) % count) for i in range(count)]
    return up, down


def shift(value, perm, axis="seq"):
    return lax.ppermute(value, axis, perm)


def ring_gather(block, count, split):
    up, down = ring_perms(count)
    mid = block.shape[0] // 2
    half = count // 2
    from_low, from_high = block, block
    low, high = [], []
    for _ in range(1, half):
        from_low = shift(from_low, up)
        from_high = shift(from_high, down)
        low.append(from_low)
        high.append(from_high)
    if split:
        far = [shift(from_low[:mid], up), shift(from_high[mid:], down)]
    else:
        far = [shift(from_low, up)]
    return [block] + low + far + high[::-1]


def ring_scatter(part, count, split):
    up, down = ring_perms(count)
    half = count // 2
    mid = part.shape[1] // 2

    def plus(mine, came):
        return (mine.astype(F32) + came.astype(F32)).astype(BF16)

    if split:
        to_low = shift(part[half, :mid], down)
        to_high = shift(part[half, mid:], up)
    else:
        to_low = shift(part[half], down)
    for step in range(half - 1, 0, -1):
        low, high = part[step], part[count - step]
        if step < half - 1:
            low, high = plus(low, to_low), plus(high, to_high)
        elif split:
            low = jnp.concatenate([plus(low[:mid], to_low), low[mid:]])
            high = jnp.concatenate([high[:mid], plus(high[mid:], to_high)])
        else:
            low = plus(low, to_low)
        low, high = lax.optimization_barrier((low, high))
        to_low = shift(low, down)
        to_high = shift(high, up)
    total = part[0].astype(F32) + to_low.astype(F32) + to_high.astype(F32)
    return total.astype(BF16)


def index_tables(meta, z, n_exp, cap):
    n_seq, double, tok = meta.shape
    topk = double // 2
    slots = cap * n_seq
    chunk = 16
    per_pair = 2 * slots // chunk

    def body(z_ref, meta_ref, pick_ref, gate_ref, code_s, weight_s):
        own = z_ref[0]
        expert = (lax.broadcasted_iota(jnp.int32, (n_exp, tok), 0) + n_exp * own).astype(F32)
        before = lax.broadcasted_iota(jnp.int32, (tok, tok), 0) < lax.broadcasted_iota(
            jnp.int32, (tok, tok), 1
        )
        before = before.astype(F32).astype(BF16)
        for p in range(n_seq):
            source = jnp.where(own >= p, own - p, own - p + n_seq)
            block = meta_ref[source]
            named = jnp.zeros((n_exp, tok), F32)
            weight = jnp.zeros((n_exp, tok), F32)
            for k in range(topk):
                hit = block[k : k + 1, :] == expert
                named = jnp.where(hit, 1.0, named)
                weight = jnp.where(hit, block[topk + k : topk + k + 1, :], weight)
            rank = jnp.dot(named.astype(BF16), before, preferred_element_type=F32)
            code = jnp.where(named > 0.0, rank + float(cap * p), -1.0)
            code_s[:, p * tok : (p + 1) * tok] = code
            weight_s[:, p * tok : (p + 1) * tok] = weight

        def pair(i, carry):
            first = code_s[pl.ds(2 * i, 1), :]
            second = code_s[pl.ds(2 * i + 1, 1), :]
            second = jnp.where(second < 0.0, -1.0, second + float(slots))
            w_first = weight_s[pl.ds(2 * i, 1), :]
            w_second = weight_s[pl.ds(2 * i + 1, 1), :]
            row = lax.broadcasted_iota(jnp.int32, (chunk, n_seq * tok), 0).astype(F32)
            for c in range(per_pair):
                here = row + float(c * chunk)
                hit_a = here == first
                hit_b = here == second
                at = pl.ds(pl.multiple_of(i * 2 * slots + c * chunk, chunk), chunk)
                pick_ref[at, :] = jnp.where(hit_a | hit_b, 1.0, 0.0).astype(BF16)
                weight = jnp.where(hit_a, w_first, 0.0) + jnp.where(hit_b, w_second, 0.0)
                gate_ref[at, :] = jnp.sum(weight, axis=1, keepdims=True)
            return carry

        lax.fori_loop(0, n_exp // 2, pair, 0)

    return pl.pallas_call(
        body,
        grid=(1,),
        in_specs=[pl.BlockSpec(memory_space=pltpu.SMEM), whole(meta.shape)],
        out_specs=[whole((n_exp * slots, n_seq * tok)), whole((n_exp * slots, 1))],
        out_shape=[
            jax.ShapeDtypeStruct((n_exp * slots, n_seq * tok), BF16),
            jax.ShapeDtypeStruct((n_exp * slots, 1), F32),
        ],
        scratch_shapes=[pltpu.VMEM((n_exp, n_seq * tok), F32)] * 2,
    )(z.reshape(1), meta)


def pick_rows(pick, pieces, cols, which=0, gate=None, block=256):
    rows = pick.shape[0]
    first = which * (cols // block)

    def body(*refs):
        out = refs[-1]
        tab = jnp.concatenate([r[...] for r in refs[1 : 1 + len(pieces)]], axis=0)
        got = jnp.dot(refs[0][...], tab, preferred_element_type=F32)
        if gate is not None:
            got = got * refs[-2][...]
        out[...] = got.astype(BF16)

    extra = [] if gate is None else [gate]
    return pl.pallas_call(
        body,
        grid=(cols // block,),
        in_specs=[whole(pick.shape)]
        + [pl.BlockSpec((p.shape[0], block), lambda j: (0, j + first)) for p in pieces]
        + [whole(g.shape) for g in extra],
        out_specs=pl.BlockSpec((rows, block), lambda j: (0, j)),
        out_shape=jax.ShapeDtypeStruct((rows, cols), BF16),
    )(pick, *pieces, *extra)


def project(x0, x1, w, block=192):
    rows, half = x0.shape
    wide = w.shape[1]

    def body(x0_ref, x1_ref, w_ref, o_ref):
        got = jnp.dot(x0_ref[...], w_ref[:half], preferred_element_type=F32)
        o_ref[...] = got + jnp.dot(x1_ref[...], w_ref[half:], preferred_element_type=F32)

    row = lambda width: pl.BlockSpec((block, width), lambda i: (i, 0))
    return pl.pallas_call(
        body,
        grid=(rows // block,),
        in_specs=[row(half), row(half), whole(w.shape)],
        out_specs=row(wide),
        out_shape=jax.ShapeDtypeStruct((rows, wide), F32),
    )(x0, x1, w)


def hidden_part(d0, wd, block=192):
    rows, half = d0.shape
    hid = wd.shape[1]

    def body(d_ref, w_ref, o_ref):
        o_ref[...] = jnp.dot(d_ref[...], w_ref[...], preferred_element_type=F32)

    row = lambda width: pl.BlockSpec((block, width), lambda i: (i, 0))
    return pl.pallas_call(
        body,
        grid=(rows // block,),
        in_specs=[row(half), pl.BlockSpec((half, hid), lambda i: (0, 0))],
        out_specs=row(hid),
        out_shape=jax.ShapeDtypeStruct((rows, hid), F32),
    )(d0, wd)


BACK_DIMS = (((1,), (1,)), ((), ()))


def middle(d1, dh0, wd, ab, w, block=384):
    rows, half = d1.shape
    hid = wd.shape[1]

    def body(d1_ref, dh_ref, wd_ref, ab_ref, w_ref, h_ref, dab_ref, back_ref):
        dh = dh_ref[...] + jnp.dot(d1_ref[...], wd_ref[...], preferred_element_type=F32)
        a, b = ab_ref[:, :hid], ab_ref[:, hid:]
        sig = jax.nn.sigmoid(a)
        act = a * sig
        h_ref[...] = (act * b).astype(BF16)
        da = (dh * b * sig * (1.0 + a * (1.0 - sig))).astype(BF16)
        db = (dh * act).astype(BF16)
        dab_ref[:, :hid] = da
        dab_ref[:, hid:] = db
        got = lax.dot_general(da, w_ref[:, :hid], BACK_DIMS, preferred_element_type=F32)
        got = got + lax.dot_general(db, w_ref[:, hid:], BACK_DIMS, preferred_element_type=F32)
        back_ref[...] = got.astype(BF16)

    row = lambda width: pl.BlockSpec((block, width), lambda i: (i, 0))
    return pl.pallas_call(
        body,
        grid=(rows // block,),
        in_specs=[
            row(half),
            row(hid),
            pl.BlockSpec((half, hid), lambda i: (1, 0)),
            row(2 * hid),
            pl.BlockSpec((half, 2 * hid), lambda i: (0, 0)),
        ],
        out_specs=[row(hid), row(2 * hid), row(half)],
        out_shape=[
            jax.ShapeDtypeStruct((rows, hid), BF16),
            jax.ShapeDtypeStruct((rows, 2 * hid), BF16),
            jax.ShapeDtypeStruct((rows, half), BF16),
        ],
    )(d1, dh0, wd, ab, w)


def back_rows(dab, w, which, block=192):
    rows, wide = dab.shape
    half = w.shape[0] // 2

    def body(d_ref, w_ref, o_ref):
        got = lax.dot_general(d_ref[...], w_ref[...], BACK_DIMS, preferred_element_type=F32)
        o_ref[...] = got.astype(BF16)

    row = lambda width: pl.BlockSpec((block, width), lambda i: (i, 0))
    return pl.pallas_call(
        body,
        grid=(rows // block,),
        in_specs=[row(wide), pl.BlockSpec((half, wide), lambda i: (which, 0))],
        out_specs=row(half),
        out_shape=jax.ShapeDtypeStruct((rows, half), BF16),
    )(dab, w)


def combine(left, right, block=256):
    rows, cols = left.shape
    dims = (((0,), (0,)), ((), ()))

    def body(l_ref, r_ref, o_ref):
        got = lax.dot_general(l_ref[...], r_ref[...], dims, preferred_element_type=F32)
        o_ref[...] = got.astype(BF16)

    return pl.pallas_call(
        body,
        grid=(cols // block,),
        in_specs=[pl.BlockSpec((rows, block), lambda j: (0, j)), whole(right.shape)],
        out_specs=pl.BlockSpec((block, right.shape[1]), lambda j: (j, 0)),
        out_shape=jax.ShapeDtypeStruct((cols, right.shape[1]), BF16),
    )(left, right)


def weight_grads(core, x0, x1, d0, d1, dab, h, block=256):
    rows, half = x0.shape
    wide = dab.shape[1]
    total = wide + h.shape[1]
    n = half // block
    dims = (((0,), (0,)), ((), ()))

    def place(j, core_ref):
        return lax.rem(j + (1 - core_ref[0]) * n, 2 * n)

    def body(core_ref, x0_ref, x1_ref, d0_ref, d1_ref, dab_ref, h_ref, other_ref, own_ref, s_ref):
        j = pl.program_id(0)
        at = place(j, core_ref)

        def fill(x_ref, d_ref):
            s_ref[0] = x_ref[...]
            s_ref[1] = d_ref[...]

        pl.when(at < n)(lambda: fill(x0_ref, d0_ref))
        pl.when(at >= n)(lambda: fill(x1_ref, d1_ref))
        ab = lax.dot_general(s_ref[0], dab_ref[...], dims, preferred_element_type=F32)
        down = lax.dot_general(s_ref[1], h_ref[...], dims, preferred_element_type=F32)

        def put(o_ref):
            o_ref[:, :wide] = ab
            o_ref[:, wide:] = down

        pl.when(j < n)(lambda: put(other_ref))
        pl.when(j >= n)(lambda: put(own_ref))

    low = pl.BlockSpec((rows, block), lambda j, c: (0, jnp.minimum(place(j, c), n - 1)))
    high = pl.BlockSpec((rows, block), lambda j, c: (0, jnp.maximum(place(j, c) - n, 0)))
    return pl.pallas_call(
        body,
        grid_spec=pltpu.PrefetchScalarGridSpec(
            num_scalar_prefetch=1,
            grid=(2 * n,),
            in_specs=[low, high, low, high, whole(dab.shape), whole(h.shape)],
            out_specs=[
                pl.BlockSpec((block, total), lambda j, c: (jnp.minimum(j, n - 1), 0)),
                pl.BlockSpec((block, total), lambda j, c: (jnp.maximum(j - n, 0), 0)),
            ],
            scratch_shapes=[pltpu.VMEM((2, rows, block), BF16)],
        ),
        out_shape=[jax.ShapeDtypeStruct((half, total), F32)] * 2,
    )(core.reshape(1), x0, x1, d0, d1, dab, h)


def finish_grad(own, came, hid, which, block=256):
    rows = own.shape[0]

    def body(own_ref, came_ref, o_ref):
        o_ref[...] = own_ref[...] + came_ref[...]

    part = pl.BlockSpec((block, hid), lambda i: (i, which))
    return pl.pallas_call(
        body,
        grid=(rows // block,),
        in_specs=[part, part],
        out_specs=pl.BlockSpec((block, hid), lambda i: (i, 0)),
        out_shape=jax.ShapeDtypeStruct((rows, hid), F32),
    )(own, came)


def on_device(tokens, route_ids, gates, d_out, w_gate, w_up, w_down):
    tok_count, width = tokens.shape
    topk = route_ids.shape[1]
    n_seq = lax.axis_size("seq")
    n_exp = lax.axis_size("exp")
    experts = n_seq * n_exp
    pairs = tok_count * topk
    cap = pairs // experts + max(1, pairs // (8 * experts))
    slots = cap * n_seq
    rows = n_exp * slots
    z = lax.axis_index("seq")
    core = lax.axis_index("edp")
    half = width // 2

    def exchange(block):
        block = block.reshape(n_exp, slots, block.shape[-1])
        got = lax.all_to_all(block, "exp", 0, 0, tiled=True)
        return got.reshape(rows, got.shape[-1])

    meta = jnp.concatenate([route_ids.T.astype(F32), gates.T], axis=0)
    meta = jnp.broadcast_to(meta[None], (n_seq,) + meta.shape)
    meta = lax.all_to_all(meta, "seq", 0, 0, tiled=True)
    tabs = {
        "x0": (ring_gather(tokens[:, :half], n_seq, True), 0),
        "x1": (ring_gather(tokens[:, half:], n_seq, False), 0),
    }
    pieces = ring_gather(d_out, n_seq, False)
    tabs["d0"] = (pieces, 0)
    tabs["d1"] = (pieces, 1)
    pick, gate = index_tables(meta, z, n_exp, cap)
    got = {}
    for name, (pieces, which) in tabs.items():
        send = pick_rows(pick, pieces, half, which, gate if name[0] == "d" else None)
        got[name] = exchange(send)
    w = jnp.concatenate([w_gate[0], w_up[0]], axis=1)
    wd = w_down[0]
    ab = project(got["x0"], got["x1"], w)
    dh0 = hidden_part(got["d0"], wd)
    hidden, d_both, back0 = middle(got["d1"], dh0, wd, ab, w)
    back1 = back_rows(d_both, w, 1)
    outs = []
    for i, back in enumerate((back0, back1)):
        back = exchange(back)
        part = combine(pick, back)
        outs.append(ring_scatter(part.reshape(n_seq, tok_count, half), n_seq, i == 1))
    d_tokens = jnp.concatenate(outs, axis=1)

    other, own = weight_grads(core, got["x0"], got["x1"], got["d0"], got["d1"], d_both, hidden)
    came = shift(other, [(0, 1), (1, 0)], "edp")
    grads = []
    for i in range(3):
        grads.append(finish_grad(own, came, wd.shape[1], i)[None])
    return (d_tokens, *grads)


def solution(mesh):
    tok = P(("seq", "exp", "edp"), None)
    wts = P(("seq", "exp"), None, None)
    out = P(("seq", "exp"), "edp", None)

    return jax.shard_map(
        on_device,
        mesh=mesh,
        in_specs=(tok, tok, tok, tok, wts, wts, wts),
        out_specs=(tok, out, out, out),
        check_vma=False,
    )
```

```python
import jax
import jax.numpy as jnp
from jax import lax
from jax.experimental import pallas as pl
from jax.experimental.pallas import tpu as pltpu
from jax.sharding import PartitionSpec as P


F32 = jnp.float32
BF16 = jnp.bfloat16


def whole(shape):
    return pl.BlockSpec(shape, lambda *_: (0,) * len(shape))


def ring_perms(count):
    up = [(i, (i + 1) % count) for i in range(count)]
    down = [(i, (i - 1) % count) for i in range(count)]
    return up, down


def shift(value, perm, axis="seq"):
    return lax.ppermute(value, axis, perm)


def ring_gather(block, count, split):
    up, down = ring_perms(count)
    mid = block.shape[0] // 2
    half = count // 2
    from_low, from_high = block, block
    low, high = [], []
    for _ in range(1, half):
        from_low = shift(from_low, up)
        from_high = shift(from_high, down)
        low.append(from_low)
        high.append(from_high)
    if split:
        far = [shift(from_low[:mid], up), shift(from_high[mid:], down)]
    else:
        far = [shift(from_low, up)]
    return [block] + low + far + high[::-1]


def ring_scatter(part, count, split):
    up, down = ring_perms(count)
    half = count // 2
    mid = part.shape[1] // 2

    def plus(mine, came):
        return (mine.astype(F32) + came.astype(F32)).astype(BF16)

    if split:
        to_low = shift(part[half, :mid], down)
        to_high = shift(part[half, mid:], up)
    else:
        to_low = shift(part[half], down)
    for step in range(half - 1, 0, -1):
        low, high = part[step], part[count - step]
        if step < half - 1:
            low, high = plus(low, to_low), plus(high, to_high)
        elif split:
            low = jnp.concatenate([plus(low[:mid], to_low), low[mid:]])
            high = jnp.concatenate([high[:mid], plus(high[mid:], to_high)])
        else:
            low = plus(low, to_low)
        low, high = lax.optimization_barrier((low, high))
        to_low = shift(low, down)
        to_high = shift(high, up)
    total = part[0].astype(F32) + to_low.astype(F32) + to_high.astype(F32)
    return total.astype(BF16)


def index_tables(meta, z, n_exp, cap):
    n_seq, double, tok = meta.shape
    topk = double // 2
    slots = cap * n_seq
    chunk = 16
    per_pair = 2 * slots // chunk

    def body(z_ref, meta_ref, pick_ref, gate_ref, code_s, weight_s):
        own = z_ref[0]
        expert = (lax.broadcasted_iota(jnp.int32, (n_exp, tok), 0) + n_exp * own).astype(F32)
        before = lax.broadcasted_iota(jnp.int32, (tok, tok), 0) < lax.broadcasted_iota(
            jnp.int32, (tok, tok), 1
        )
        before = before.astype(F32).astype(BF16)
        for p in range(n_seq):
            source = jnp.where(own >= p, own - p, own - p + n_seq)
            block = meta_ref[source]
            named = jnp.zeros((n_exp, tok), F32)
            weight = jnp.zeros((n_exp, tok), F32)
            for k in range(topk):
                hit = block[k : k + 1, :] == expert
                named = jnp.where(hit, 1.0, named)
                weight = jnp.where(hit, block[topk + k : topk + k + 1, :], weight)
            rank = jnp.dot(named.astype(BF16), before, preferred_element_type=F32)
            code = jnp.where(named > 0.0, rank + float(cap * p), -1.0)
            code_s[:, p * tok : (p + 1) * tok] = code
            weight_s[:, p * tok : (p + 1) * tok] = weight

        def pair(i, carry):
            first = code_s[pl.ds(2 * i, 1), :]
            second = code_s[pl.ds(2 * i + 1, 1), :]
            second = jnp.where(second < 0.0, -1.0, second + float(slots))
            w_first = weight_s[pl.ds(2 * i, 1), :]
            w_second = weight_s[pl.ds(2 * i + 1, 1), :]
            row = lax.broadcasted_iota(jnp.int32, (chunk, n_seq * tok), 0).astype(F32)
            for c in range(per_pair):
                here = row + float(c * chunk)
                hit_a = here == first
                hit_b = here == second
                at = pl.ds(pl.multiple_of(i * 2 * slots + c * chunk, chunk), chunk)
                pick_ref[at, :] = jnp.where(hit_a | hit_b, 1.0, 0.0).astype(BF16)
                weight = jnp.where(hit_a, w_first, 0.0) + jnp.where(hit_b, w_second, 0.0)
                gate_ref[at, :] = jnp.sum(weight, axis=1, keepdims=True)
            return carry

        lax.fori_loop(0, n_exp // 2, pair, 0)

    return pl.pallas_call(
        body,
        grid=(1,),
        in_specs=[pl.BlockSpec(memory_space=pltpu.SMEM), whole(meta.shape)],
        out_specs=[whole((n_exp * slots, n_seq * tok)), whole((n_exp * slots, 1))],
        out_shape=[
            jax.ShapeDtypeStruct((n_exp * slots, n_seq * tok), BF16),
            jax.ShapeDtypeStruct((n_exp * slots, 1), F32),
        ],
        scratch_shapes=[pltpu.VMEM((n_exp, n_seq * tok), F32)] * 2,
    )(z.reshape(1), meta)


def pick_rows(pick, pieces, gate=None, block=256):
    rows, cols = pick.shape[0], pieces[0].shape[1]

    def body(*refs):
        out = refs[-1]
        tab = jnp.concatenate([r[...] for r in refs[1 : 1 + len(pieces)]], axis=0)
        got = jnp.dot(refs[0][...], tab, preferred_element_type=F32)
        if gate is not None:
            got = got * refs[-2][...]
        out[...] = got.astype(BF16)

    extra = [] if gate is None else [gate]
    return pl.pallas_call(
        body,
        grid=(cols // block,),
        in_specs=[whole(pick.shape)]
        + [pl.BlockSpec((p.shape[0], block), lambda j: (0, j)) for p in pieces]
        + [whole(g.shape) for g in extra],
        out_specs=pl.BlockSpec((rows, block), lambda j: (0, j)),
        out_shape=jax.ShapeDtypeStruct((rows, cols), BF16),
    )(pick, *pieces, *extra)


def project(x0, x1, w, block=192):
    rows, half = x0.shape
    wide = w.shape[1]

    def body(x0_ref, x1_ref, w_ref, o_ref):
        got = jnp.dot(x0_ref[...], w_ref[:half], preferred_element_type=F32)
        o_ref[...] = got + jnp.dot(x1_ref[...], w_ref[half:], preferred_element_type=F32)

    row = lambda width: pl.BlockSpec((block, width), lambda i: (i, 0))
    return pl.pallas_call(
        body,
        grid=(rows // block,),
        in_specs=[row(half), row(half), whole(w.shape)],
        out_specs=row(wide),
        out_shape=jax.ShapeDtypeStruct((rows, wide), F32),
    )(x0, x1, w)


def hidden_part(d0, wd, block=192):
    rows, half = d0.shape
    hid = wd.shape[1]

    def body(d_ref, w_ref, o_ref):
        o_ref[...] = jnp.dot(d_ref[...], w_ref[...], preferred_element_type=F32)

    row = lambda width: pl.BlockSpec((block, width), lambda i: (i, 0))
    return pl.pallas_call(
        body,
        grid=(rows // block,),
        in_specs=[row(half), pl.BlockSpec((half, hid), lambda i: (0, 0))],
        out_specs=row(hid),
        out_shape=jax.ShapeDtypeStruct((rows, hid), F32),
    )(d0, wd)


BACK_DIMS = (((1,), (1,)), ((), ()))


def middle(d1, dh0, wd, ab, w, block=384):
    rows, half = d1.shape
    hid = wd.shape[1]

    def body(d1_ref, dh_ref, wd_ref, ab_ref, w_ref, h_ref, dab_ref, back_ref):
        dh = dh_ref[...] + jnp.dot(d1_ref[...], wd_ref[...], preferred_element_type=F32)
        a, b = ab_ref[:, :hid], ab_ref[:, hid:]
        sig = jax.nn.sigmoid(a)
        act = a * sig
        h_ref[...] = (act * b).astype(BF16)
        da = (dh * b * sig * (1.0 + a * (1.0 - sig))).astype(BF16)
        db = (dh * act).astype(BF16)
        dab_ref[:, :hid] = da
        dab_ref[:, hid:] = db
        got = lax.dot_general(da, w_ref[:, :hid], BACK_DIMS, preferred_element_type=F32)
        got = got + lax.dot_general(db, w_ref[:, hid:], BACK_DIMS, preferred_element_type=F32)
        back_ref[...] = got.astype(BF16)

    row = lambda width: pl.BlockSpec((block, width), lambda i: (i, 0))
    return pl.pallas_call(
        body,
        grid=(rows // block,),
        in_specs=[
            row(half),
            row(hid),
            pl.BlockSpec((half, hid), lambda i: (1, 0)),
            row(2 * hid),
            pl.BlockSpec((half, 2 * hid), lambda i: (0, 0)),
        ],
        out_specs=[row(hid), row(2 * hid), row(half)],
        out_shape=[
            jax.ShapeDtypeStruct((rows, hid), BF16),
            jax.ShapeDtypeStruct((rows, 2 * hid), BF16),
            jax.ShapeDtypeStruct((rows, half), BF16),
        ],
    )(d1, dh0, wd, ab, w)


def back_rows(dab, w, which, block=192):
    rows, wide = dab.shape
    half = w.shape[0] // 2

    def body(d_ref, w_ref, o_ref):
        got = lax.dot_general(d_ref[...], w_ref[...], BACK_DIMS, preferred_element_type=F32)
        o_ref[...] = got.astype(BF16)

    row = lambda width: pl.BlockSpec((block, width), lambda i: (i, 0))
    return pl.pallas_call(
        body,
        grid=(rows // block,),
        in_specs=[row(wide), pl.BlockSpec((half, wide), lambda i: (which, 0))],
        out_specs=row(half),
        out_shape=jax.ShapeDtypeStruct((rows, half), BF16),
    )(dab, w)


def combine(left, right, block=256):
    rows, cols = left.shape
    dims = (((0,), (0,)), ((), ()))

    def body(l_ref, r_ref, o_ref):
        got = lax.dot_general(l_ref[...], r_ref[...], dims, preferred_element_type=F32)
        o_ref[...] = got.astype(BF16)

    return pl.pallas_call(
        body,
        grid=(cols // block,),
        in_specs=[pl.BlockSpec((rows, block), lambda j: (0, j)), whole(right.shape)],
        out_specs=pl.BlockSpec((block, right.shape[1]), lambda j: (j, 0)),
        out_shape=jax.ShapeDtypeStruct((cols, right.shape[1]), BF16),
    )(left, right)


def weight_grads(core, x0, x1, d0, d1, dab, h, block=256):
    rows, half = x0.shape
    wide = dab.shape[1]
    total = wide + h.shape[1]
    n = half // block
    dims = (((0,), (0,)), ((), ()))

    def place(j, core_ref):
        return lax.rem(j + (1 - core_ref[0]) * n, 2 * n)

    def body(core_ref, x0_ref, x1_ref, d0_ref, d1_ref, dab_ref, h_ref, other_ref, own_ref, s_ref):
        j = pl.program_id(0)
        at = place(j, core_ref)

        def fill(x_ref, d_ref):
            s_ref[0] = x_ref[...]
            s_ref[1] = d_ref[...]

        pl.when(at < n)(lambda: fill(x0_ref, d0_ref))
        pl.when(at >= n)(lambda: fill(x1_ref, d1_ref))
        ab = lax.dot_general(s_ref[0], dab_ref[...], dims, preferred_element_type=F32)
        down = lax.dot_general(s_ref[1], h_ref[...], dims, preferred_element_type=F32)

        def put(o_ref):
            o_ref[:, :wide] = ab
            o_ref[:, wide:] = down

        pl.when(j < n)(lambda: put(other_ref))
        pl.when(j >= n)(lambda: put(own_ref))

    low = pl.BlockSpec((rows, block), lambda j, c: (0, jnp.minimum(place(j, c), n - 1)))
    high = pl.BlockSpec((rows, block), lambda j, c: (0, jnp.maximum(place(j, c) - n, 0)))
    return pl.pallas_call(
        body,
        grid_spec=pltpu.PrefetchScalarGridSpec(
            num_scalar_prefetch=1,
            grid=(2 * n,),
            in_specs=[low, high, low, high, whole(dab.shape), whole(h.shape)],
            out_specs=[
                pl.BlockSpec((block, total), lambda j, c: (jnp.minimum(j, n - 1), 0)),
                pl.BlockSpec((block, total), lambda j, c: (jnp.maximum(j - n, 0), 0)),
            ],
            scratch_shapes=[pltpu.VMEM((2, rows, block), BF16)],
        ),
        out_shape=[jax.ShapeDtypeStruct((half, total), F32)] * 2,
    )(core.reshape(1), x0, x1, d0, d1, dab, h)


def finish_grad(own, came, hid, which, block=256):
    rows = own.shape[0]

    def body(own_ref, came_ref, o_ref):
        o_ref[...] = own_ref[...] + came_ref[...]

    part = pl.BlockSpec((block, hid), lambda i: (i, which))
    return pl.pallas_call(
        body,
        grid=(rows // block,),
        in_specs=[part, part],
        out_specs=pl.BlockSpec((block, hid), lambda i: (i, 0)),
        out_shape=jax.ShapeDtypeStruct((rows, hid), F32),
    )(own, came)


def on_device(tokens, route_ids, gates, d_out, w_gate, w_up, w_down):
    tok_count, width = tokens.shape
    topk = route_ids.shape[1]
    n_seq = lax.axis_size("seq")
    n_exp = lax.axis_size("exp")
    experts = n_seq * n_exp
    pairs = tok_count * topk
    cap = pairs // experts + max(1, pairs // (8 * experts))
    slots = cap * n_seq
    rows = n_exp * slots
    z = lax.axis_index("seq")
    core = lax.axis_index("edp")
    half = width // 2

    def exchange(block):
        block = block.reshape(n_exp, slots, block.shape[-1])
        got = lax.all_to_all(block, "exp", 0, 0, tiled=True)
        return got.reshape(rows, got.shape[-1])

    meta = jnp.concatenate([route_ids.T.astype(F32), gates.T], axis=0)
    meta = jnp.broadcast_to(meta[None], (n_seq,) + meta.shape)
    meta = lax.all_to_all(meta, "seq", 0, 0, tiled=True)
    tabs = {
        "x0": ring_gather(tokens[:, :half], n_seq, True),
        "x1": ring_gather(tokens[:, half:], n_seq, True),
    }
    tabs["d0"] = ring_gather(d_out[:, :half], n_seq, True)
    tabs["d1"] = ring_gather(d_out[:, half:], n_seq, False)
    pick, gate = index_tables(meta, z, n_exp, cap)
    got = {}
    for name, pieces in tabs.items():
        send = pick_rows(pick, pieces, gate if name[0] == "d" else None)
        got[name] = exchange(send)
    w = jnp.concatenate([w_gate[0], w_up[0]], axis=1)
    wd = w_down[0]
    ab = project(got["x0"], got["x1"], w)
    dh0 = hidden_part(got["d0"], wd)
    hidden, d_both, back0 = middle(got["d1"], dh0, wd, ab, w)
    back1 = back_rows(d_both, w, 1)
    outs = []
    for i, back in enumerate((back0, back1)):
        back = exchange(back)
        part = combine(pick, back)
        outs.append(ring_scatter(part.reshape(n_seq, tok_count, half), n_seq, i == 1))
    d_tokens = jnp.concatenate(outs, axis=1)

    other, own = weight_grads(core, got["x0"], got["x1"], got["d0"], got["d1"], d_both, hidden)
    came = shift(other, [(0, 1), (1, 0)], "edp")
    grads = []
    for i in range(3):
        grads.append(finish_grad(own, came, wd.shape[1], i)[None])
    return (d_tokens, *grads)


def solution(mesh):
    tok = P(("seq", "exp", "edp"), None)
    wts = P(("seq", "exp"), None, None)
    out = P(("seq", "exp"), "edp", None)

    return jax.shard_map(
        on_device,
        mesh=mesh,
        in_specs=(tok, tok, tok, tok, wts, wts, wts),
        out_specs=(tok, out, out, out),
        check_vma=False,
    )
```
